768 devices in a mesh: grp: 192 (over x, y_lo, z), tp: 4 (over y_hi, core).
Axes of the slice: x: 4, y: 8 (y_hi: 2, y_lo: 4; y = y_hi * 4 + y_lo), z: 12, core: 2. Of those that a mesh axis runs over, the one named last changes fastest.
Arguments:
- activations: bfloat16 [49152, 5120], P('grp', 'tp'), may hold values from -6 to 6
- cotangent: bfloat16 [49152, 512], P('grp'), may hold values from -1.5 to 1.5
- advantage: int32 [192], replicated, may hold values from -512 to 512
- seq_len: int32 [192], replicated, may hold values from 64 to 256, as said below
- key_master: float32 [4, 1344, 512], P('tp', 'grp'), may hold values from -0.078125 to 0.078125
- moment_one: float32 [4, 1344, 512], P('tp', 'grp'), may hold values from -3 to 3
- moment_two: float32 [4, 1344, 512], P('tp', 'grp'), may hold values from 0.1 to 2
- decode_hidden: bfloat16 [192, 4, 5120], P('grp'), may hold values from -6 to 6
- queries: bfloat16 [192, 4, 2560], P('grp', None, 'tp'), may hold values from -34 to 34
- cache_keys: bfloat16 [192, 2048, 512], P('grp', None, 'tp'), may hold values from -6 to 6
- cache_values: bfloat16 [192, 2048, 512], P('grp', None, 'tp'), may hold values from -6 to 6
- cache_len: int32 [192], P('grp'), may hold values from 2 to 2048, as said below
- value_weight: bfloat16 [5120, 512], P(None, 'tp'), may hold values from -0.078125 to 0.078125
Outputs:
- master_new: float32 [4, 1344, 512], P('tp', 'grp')
- moment_one_new: float32 [4, 1344, 512], P('tp', 'grp')
- moment_two_new: float32 [4, 1344, 512], P('tp', 'grp')
- new_keys: bfloat16 [192, 4, 512], P('grp', None, 'tp')
- new_values: bfloat16 [192, 4, 512], P('grp', None, 'tp')
- attention: bfloat16 [192, 4, 2560], P('grp', None, 'tp')
The draws below stay inside these ranges and needn't reach their ends.
Inputs may be any that keep to these rules, and one draw needn't show every extreme that they name: `seq_len`: the first sequence is full. `cache_len`: row 0 has a full cache.
All inputs are finite; a program needn't handle non-finite values.
Results may differ from the reference program's by a relative error of at most 0.0044.
The reference program's roundings to bfloat16 on the way count: a program that leaves them out, or rounds other values in their place, can miss the bound.
Values may be sent and summed in bfloat16 or wider, within the bound.
No kernel may reach another device: no remote copies, remote signals or barrier semaphores. Data moves between devices by JAX's collectives and lax.ppermute only.
A program may use at most 32 MiB of HBM per device.

```python
import math
import jax
import jax.numpy as jnp
from jax import lax

D = 5120
HD = 128
KVH = 4
GQA = 5
STEPS = 4
CACHE = 2048
SEQ = 256
QH = 20
KW = 512
DQ = 1280
DQPAD = 1344
TOKENS = 49152
NSEQ = 192
ROWS = 192
N_TP = 4


def shared_cache(key):
    base = jax.random.fold_in(key, 11)
    keys = jnp.clip(jax.random.normal(base, (ROWS, CACHE, KW), jnp.float32), -6.0, 6.0)
    return keys


def draw_cache_keys(key, part):
    return shared_cache(key).astype(jnp.bfloat16)


def draw_queries(key, part):
    own = jax.random.fold_in(key, 23)
    values = jnp.clip(jax.random.normal(own, (ROWS, STEPS, QH * HD), jnp.float32), -6.0, 6.0)
    return values.astype(jnp.bfloat16)


def draw_seq_len(key, part):
    lengths = jax.random.randint(jax.random.fold_in(key, 31), (NSEQ,), SEQ // 4, SEQ + 1)
    return lengths.at[0].set(SEQ).astype(jnp.int32)


def draw_cache_len(key, part):
    lengths = jax.random.randint(jax.random.fold_in(key, 37), (ROWS,), 2, CACHE + 1)
    return lengths.at[0].set(CACHE).astype(jnp.int32)


def plant(drawn, key, smallest, high):
    longest = drawn.shape.index(max(drawn.shape))
    spots = []
    for shift in (0, 1):
        where = [jax.random.randint(jax.random.fold_in(key, axis), (), 0, length) for axis, length in enumerate(drawn.shape)]
        where[longest] = (where[longest] + shift) % drawn.shape[longest]
        spots.append(tuple(where))
    return drawn.at[spots[0]].set(smallest).at[spots[1]].set(high)


def block_scale(key, shape, shards, low, high):
    def one(dim, blocks):
        heights = jax.random.uniform(jax.random.fold_in(jax.random.fold_in(key, 6), dim), (blocks,), jnp.float32, low / len(shards), high / len(shards))
        return jnp.repeat(jnp.exp(heights), shape[dim] // blocks).reshape((-1,) + (1,) * (len(shape) - dim - 1))

    gain = one(*shards[0])
    for cut in shards[1:]:
        gain = gain * one(*cut)
    return gain


def scatter_about(own_key, dims, scale, bound, cuts=(), kind=jnp.bfloat16):
    result = jax.random.normal(own_key, dims, jnp.float32) * scale
    if len(cuts) > 0:
        result = block_scale(own_key, dims, cuts, -0.22, 0.18) * result
    return jnp.clip(result, min=-bound, max=bound).astype(kind)


def setup_inputs(seed: int = 0) -> dict:
    arg_keys = jax.random.split(jax.random.key(seed), 14)
    activations = scatter_about(arg_keys[0], (TOKENS, D), 1.0, 6.0, ((0, 192), (1, 4)))
    cotangent = scatter_about(arg_keys[1], (TOKENS, KW), 0.25, 1.5, ((0, 192),))
    advantage = plant(jax.random.randint(arg_keys[2], (NSEQ,), -512, 513), jax.random.fold_in(arg_keys[2], 1), -512, 512).astype(jnp.int32)
    seq_len = draw_seq_len(jax.random.fold_in(arg_keys[13], 71), 0)
    key_master = scatter_about(arg_keys[4], (N_TP, DQPAD, KW), D ** -0.5, 0.078125, ((0, 4), (1, 192)), jnp.float32)
    moment_one = scatter_about(arg_keys[5], (N_TP, DQPAD, KW), 0.5, 3.0, ((0, 4), (1, 192)), jnp.float32)
    moment_two = jnp.clip(jnp.exp(math.log(2.0) - 2.9957323 * jax.random.uniform(arg_keys[6], (N_TP, DQPAD, KW), jnp.float32) ** block_scale(arg_keys[6], (N_TP, DQPAD, KW), ((0, 4), (1, 192)), -0.2, 0.2)), 0.1, 2.0)
    decode_hidden = scatter_about(arg_keys[7], (ROWS, STEPS, D), 1.0, 6.0, ((0, 192),))
    queries = draw_queries(jax.random.fold_in(arg_keys[13], 71), 0)
    cache_keys = draw_cache_keys(jax.random.fold_in(arg_keys[13], 71), 0)
    cache_values = scatter_about(arg_keys[10], (ROWS, CACHE, KW), 1.0, 6.0, ((0, 192), (2, 4)))
    cache_len = draw_cache_len(jax.random.fold_in(arg_keys[13], 71), 0)
    value_weight = scatter_about(arg_keys[12], (D, KW), D ** -0.5, 0.078125, ((1, 4),))
    return dict(activations=activations, cotangent=cotangent, advantage=advantage, seq_len=seq_len, key_master=key_master, moment_one=moment_one, moment_two=moment_two, decode_hidden=decode_hidden, queries=queries, cache_keys=cache_keys, cache_values=cache_values, cache_len=cache_len, value_weight=value_weight)


def reference(activations, cotangent, advantage, seq_len, key_master, moment_one, moment_two, decode_hidden, queries, cache_keys, cache_values, cache_len, value_weight):
    position = jnp.arange(TOKENS, dtype=jnp.int32)
    seq_index = position // SEQ
    within = position % SEQ
    length_tok = seq_len[seq_index]
    adv_tok = advantage[seq_index].astype(jnp.float32) / 256.0
    scale = jnp.where(within < length_tok, adv_tok, jnp.float32(0.0)) / NSEQ
    weighted = (cotangent.astype(jnp.float32) * scale[:, None]).astype(jnp.bfloat16)
    gradient = jnp.dot(activations.T, weighted, preferred_element_type=jnp.float32)
    grad_blocks = gradient.reshape(N_TP, DQ, KW)
    grad_blocks = jnp.concatenate([grad_blocks, jnp.zeros((N_TP, DQPAD - DQ, KW), jnp.float32)], axis=1)
    corr_one = 1.0 - 0.9 ** 10
    corr_two = 1.0 - 0.95 ** 10
    moment_one_new = 0.9 * moment_one + 0.1 * grad_blocks
    moment_two_new = 0.95 * moment_two + 0.05 * grad_blocks * grad_blocks
    master_new = key_master - 0.005 * (moment_one_new / corr_one) / (jnp.sqrt(moment_two_new / corr_two) + 1e-08)
    relayed = master_new.astype(jnp.bfloat16)[:, :DQ, :].reshape(D, KW)
    flat_hidden = decode_hidden.reshape(ROWS * STEPS, D)
    new_keys = jnp.dot(flat_hidden, relayed, preferred_element_type=jnp.float32).astype(jnp.bfloat16).reshape(ROWS, STEPS, KW)
    new_values = jnp.dot(flat_hidden, value_weight, preferred_element_type=jnp.float32).astype(jnp.bfloat16).reshape(ROWS, STEPS, KW)
    inverse = 1.0 / math.sqrt(HD)
    shaped_q = queries.astype(jnp.float32).reshape(ROWS, STEPS, KVH, GQA, HD)
    keys_c = cache_keys.astype(jnp.float32).reshape(ROWS, CACHE, KVH, HD)
    vals_c = cache_values.astype(jnp.float32).reshape(ROWS, CACHE, KVH, HD)
    keys_n = new_keys.astype(jnp.float32).reshape(ROWS, STEPS, KVH, HD)
    vals_n = new_values.astype(jnp.float32).reshape(ROWS, STEPS, KVH, HD)
    score_c = jnp.einsum('rsgqd,rcgd->rgsqc', shaped_q, keys_c) * inverse
    score_n = jnp.einsum('rsgqd,rtgd->rgsqt', shaped_q, keys_n) * inverse
    valid = jnp.arange(CACHE, dtype=jnp.int32)[None, :] < cache_len[:, None]
    score_c = jnp.where(valid[:, None, None, None, :], score_c, -jnp.inf)
    causal = jnp.arange(STEPS, dtype=jnp.int32)[None, :] <= jnp.arange(STEPS, dtype=jnp.int32)[:, None]
    score_n = jnp.where(causal[None, None, :, None, :], score_n, -jnp.inf)
    top = jnp.maximum(lax.optimization_barrier(jnp.max(score_c, axis=-1)), lax.optimization_barrier(jnp.max(score_n, axis=-1)))
    exp_c = jnp.exp(score_c - top[..., None])
    exp_n = jnp.exp(score_n - top[..., None])
    total = lax.optimization_barrier(jnp.sum(exp_c, axis=-1)) + lax.optimization_barrier(jnp.sum(exp_n, axis=-1))
    probs_c = (exp_c / total[..., None]).astype(jnp.bfloat16).astype(jnp.float32)
    probs_n = (exp_n / total[..., None]).astype(jnp.bfloat16).astype(jnp.float32)
    mixed = jnp.einsum('rgsqc,rcgd->rsgqd', probs_c, vals_c) + jnp.einsum('rgsqt,rtgd->rsgqd', probs_n, vals_n)
    attention = mixed.astype(jnp.bfloat16).reshape(ROWS, STEPS, QH * HD)
    return (master_new, moment_one_new, moment_two_new, new_keys, new_values, attention)
```

```python
import math

import jax
import jax.numpy as jnp
from jax import lax
from jax.sharding import Mesh, PartitionSpec as P

HD = 128
GQA = 5
SEQ = 256
NX, NY, NZ = 4, 4, 12
OWN = 7
PAD = 8
TP = 4


def attend(queries, cache_keys, cache_values, cache_len, new_keys, new_values):
    rows, steps, width = queries.shape
    length = cache_keys.shape[1]
    heads_kv = cache_keys.shape[2] // HD
    inverse = 1.0 / math.sqrt(HD)
    shaped_q = queries.reshape(rows, steps, heads_kv, GQA, HD)
    keys_c = cache_keys.reshape(rows, length, heads_kv, HD)
    vals_c = cache_values.reshape(rows, length, heads_kv, HD)
    keys_n = new_keys.reshape(rows, steps, heads_kv, HD)
    vals_n = new_values.reshape(rows, steps, heads_kv, HD)
    score_c = (
        jnp.einsum("rsgqd,rcgd->rgsqc", shaped_q, keys_c, preferred_element_type=jnp.float32)
        * inverse
    )
    score_n = (
        jnp.einsum("rsgqd,rtgd->rgsqt", shaped_q, keys_n, preferred_element_type=jnp.float32)
        * inverse
    )
    valid = jnp.arange(length, dtype=jnp.int32)[None, :] < cache_len[:, None]
    score_c = jnp.where(valid[:, None, None, None, :], score_c, -jnp.inf)
    causal = (
        jnp.arange(steps, dtype=jnp.int32)[None, :] <= jnp.arange(steps, dtype=jnp.int32)[:, None]
    )
    score_n = jnp.where(causal[None, None, :, None, :], score_n, -jnp.inf)
    top = jnp.maximum(jnp.max(score_c, axis=-1), jnp.max(score_n, axis=-1))
    exp_c = jnp.exp(score_c - top[..., None])
    exp_n = jnp.exp(score_n - top[..., None])
    total = jnp.sum(exp_c, axis=-1) + jnp.sum(exp_n, axis=-1)
    probs_c = (exp_c / total[..., None]).astype(jnp.bfloat16)
    probs_n = (exp_n / total[..., None]).astype(jnp.bfloat16)
    mixed = jnp.einsum("rgsqc,rcgd->rsgqd", probs_c, vals_c, preferred_element_type=jnp.float32)
    mixed = mixed + jnp.einsum(
        "rgsqt,rtgd->rsgqd", probs_n, vals_n, preferred_element_type=jnp.float32
    )
    return mixed.astype(jnp.bfloat16).reshape(rows, steps, width)


def pick(rows, cols, source):
    r = lax.broadcasted_iota(jnp.int32, (rows, cols), 0)
    c = lax.broadcasted_iota(jnp.int32, (rows, cols), 1)
    return source(r, c).astype(jnp.bfloat16)


def shards(
    activations,
    cotangent,
    advantage,
    seq_len,
    key_master,
    moment_one,
    moment_two,
    decode_hidden,
    queries,
    cache_keys,
    cache_values,
    cache_len,
    value_weight,
):
    bf16, f32 = jnp.bfloat16, jnp.float32
    tok_rows, quarter_rows = activations.shape
    sequences = seq_len.shape[0]
    padded_rows = OWN * NX * NY * NZ
    group = lax.axis_index(("x", "y", "z"))
    within = jnp.arange(tok_rows, dtype=jnp.int32)
    length = lax.dynamic_index_in_dim(seq_len, group, keepdims=False)
    adv = lax.dynamic_index_in_dim(advantage, group, keepdims=False).astype(f32) / 256.0
    scale = jnp.where(within < length, adv, f32(0.0)) / sequences
    weighted = (cotangent.astype(f32) * scale[:, None]).astype(bf16)
    padded = jnp.pad(activations, ((0, 0), (0, padded_rows - quarter_rows)))
    partial = lax.dot_general(
        padded, weighted, (((0,), (0,)), ((), ())), preferred_element_type=f32
    ).astype(bf16)
    width = partial.shape[1]

    steps = decode_hidden.shape[1]
    by_quarter = jnp.pad(
        decode_hidden.reshape(steps * TP, quarter_rows), ((0, 0), (0, padded_rows - quarter_rows))
    )
    span = OWN * NZ
    spread = pick(
        padded_rows,
        NZ * NX * NY * PAD,
        lambda r, c: (r // span == (c // PAD) % (NX * NY))
        & (r % span // OWN == c // (NX * NY * PAD))
        & (r % OWN == c % PAD),
    )
    placed_h = jnp.dot(by_quarter, spread, preferred_element_type=f32).astype(bf16)
    placed_h = placed_h.reshape(steps, TP, NZ, HD).transpose(2, 0, 1, 3).reshape(NZ, steps, TP * HD)
    placed_h = jnp.pad(placed_h, ((0, 0), (0, PAD - steps), (0, 0)))

    got = lax.all_to_all(partial, "x", 0, 0, tiled=True)
    part_x = jnp.sum(got.reshape(NX, -1, width).astype(f32), axis=0).astype(bf16)
    blocks = NY * NZ
    stretch = pick(
        blocks * PAD, blocks * OWN, lambda r, c: (r // PAD == c // OWN) & (r % PAD == c % OWN)
    )
    part_x = jnp.dot(stretch, part_x, preferred_element_type=f32).astype(bf16)
    got = lax.all_to_all(part_x, "y", 0, 0, tiled=True)
    part_y = jnp.sum(got.reshape(NY, -1, width).astype(f32), axis=0).astype(bf16)
    packed = jnp.concatenate([part_y.reshape(NZ, PAD, width), placed_h], axis=1)
    got = lax.all_to_all(packed.reshape(NZ * 2 * PAD, width), "z", 0, 0, tiled=True)
    got = got.reshape(NZ, 2 * PAD, width)
    gradient = jnp.sum(got[:, :OWN].astype(f32), axis=0).reshape(key_master.shape)
    hidden_z = got[:, PAD : PAD + steps].reshape(NZ * steps, width)

    corr_one = 1.0 - 0.9**10
    corr_two = 1.0 - 0.95**10
    moment_one_new = 0.9 * moment_one + 0.1 * gradient
    moment_two_new = 0.95 * moment_two + 0.05 * gradient * gradient
    master_new = key_master - 0.005 * (moment_one_new / corr_one) / (
        jnp.sqrt(moment_two_new / corr_two) + 1e-08
    )
    relay = jnp.pad(master_new[0].astype(bf16), ((0, PAD - OWN), (0, 0)))

    heads = relay.reshape(PAD, TP, HD).transpose(1, 0, 2)
    send = jnp.broadcast_to(heads[None], (NX * NY, TP, PAD, HD)).reshape(-1, HD)
    got = lax.all_to_all(send, ("x", "y", "h", "c"), 0, 0, tiled=True)
    weight = got.reshape(NX * NY, TP, PAD, HD).transpose(1, 0, 2, 3).reshape(-1, HD)
    keys_z = jnp.dot(hidden_z, weight, preferred_element_type=f32)
    got = lax.all_to_all(keys_z.reshape(NZ, steps, HD), "z", 0, 0, tiled=True)
    new_keys = jnp.sum(got, axis=0).astype(bf16)[None]

    flat_hidden = decode_hidden.reshape(steps, -1)
    new_values = jnp.dot(flat_hidden, value_weight, preferred_element_type=f32).astype(bf16)[None]
    attention = attend(queries, cache_keys, cache_values, cache_len, new_keys, new_values)
    return (master_new, moment_one_new, moment_two_new, new_keys, new_values, attention)


def solution(mesh):
    grid = Mesh(mesh.devices.reshape(NX, NY, NZ, 2, 2), ("x", "y", "z", "h", "c"))
    grp, tp = ("x", "y", "z"), ("h", "c")
    placed = (
        P(grp, tp),
        P(grp, None),
        P(),
        P(),
        P(tp, grp, None),
        P(tp, grp, None),
        P(tp, grp, None),
        P(grp, None, None),
        P(grp, None, tp),
        P(grp, None, tp),
        P(grp, None, tp),
        P(grp),
        P(None, tp),
    )
    return jax.shard_map(
        shards,
        mesh=grid,
        in_specs=placed,
        out_specs=(
            P(tp, grp, None),
            P(tp, grp, None),
            P(tp, grp, None),
            P(grp, None, tp),
            P(grp, None, tp),
            P(grp, None, tp),
        ),
        check_vma=False,
    )
```

```python
import math

import jax
import jax.numpy as jnp
from jax import lax
from jax.sharding import Mesh, PartitionSpec as P

HD = 128
GQA = 5
SEQ = 256
NX, NY, NZ = 4, 4, 12
OWN = 7
PAD = 8
TP = 4


def attend(queries, cache_keys, cache_values, cache_len, new_keys, new_values):
    rows, steps, width = queries.shape
    length = cache_keys.shape[1]
    heads_kv = cache_keys.shape[2] // HD
    inverse = 1.0 / math.sqrt(HD)
    shaped_q = queries.reshape(rows, steps, heads_kv, GQA, HD)
    keys_c = cache_keys.reshape(rows, length, heads_kv, HD)
    vals_c = cache_values.reshape(rows, length, heads_kv, HD)
    keys_n = new_keys.reshape(rows, steps, heads_kv, HD)
    vals_n = new_values.reshape(rows, steps, heads_kv, HD)
    score_c = (
        jnp.einsum("rsgqd,rcgd->rgsqc", shaped_q, keys_c, preferred_element_type=jnp.float32)
        * inverse
    )
    score_n = (
        jnp.einsum("rsgqd,rtgd->rgsqt", shaped_q, keys_n, preferred_element_type=jnp.float32)
        * inverse
    )
    valid = jnp.arange(length, dtype=jnp.int32)[None, :] < cache_len[:, None]
    score_c = jnp.where(valid[:, None, None, None, :], score_c, -jnp.inf)
    causal = (
        jnp.arange(steps, dtype=jnp.int32)[None, :] <= jnp.arange(steps, dtype=jnp.int32)[:, None]
    )
    score_n = jnp.where(causal[None, None, :, None, :], score_n, -jnp.inf)
    top = jnp.maximum(jnp.max(score_c, axis=-1), jnp.max(score_n, axis=-1))
    exp_c = jnp.exp(score_c - top[..., None])
    exp_n = jnp.exp(score_n - top[..., None])
    total = jnp.sum(exp_c, axis=-1) + jnp.sum(exp_n, axis=-1)
    probs_c = (exp_c / total[..., None]).astype(jnp.bfloat16)
    probs_n = (exp_n / total[..., None]).astype(jnp.bfloat16)
    mixed = jnp.einsum("rgsqc,rcgd->rsgqd", probs_c, vals_c, preferred_element_type=jnp.float32)
    mixed = mixed + jnp.einsum(
        "rgsqt,rtgd->rsgqd", probs_n, vals_n, preferred_element_type=jnp.float32
    )
    return mixed.astype(jnp.bfloat16).reshape(rows, steps, width)


def pick(rows, cols, source):
    r = lax.broadcasted_iota(jnp.int32, (rows, cols), 0)
    c = lax.broadcasted_iota(jnp.int32, (rows, cols), 1)
    return source(r, c).astype(jnp.bfloat16)


def shards(
    activations,
    cotangent,
    advantage,
    seq_len,
    key_master,
    moment_one,
    moment_two,
    decode_hidden,
    queries,
    cache_keys,
    cache_values,
    cache_len,
    value_weight,
):
    bf16, f32 = jnp.bfloat16, jnp.float32
    tok_rows, quarter_rows = activations.shape
    sequences = seq_len.shape[0]
    padded_rows = OWN * NX * NY * NZ
    group = lax.axis_index(("x", "y", "z"))
    within = jnp.arange(tok_rows, dtype=jnp.int32)
    mine = jnp.arange(sequences, dtype=jnp.int32) == group
    length = jnp.sum(jnp.where(mine, seq_len, 0))
    adv = jnp.sum(jnp.where(mine, advantage, 0)).astype(f32) / 256.0
    scale = jnp.where(within < length, adv, f32(0.0)) / sequences
    weighted = (cotangent.astype(f32) * scale[:, None]).astype(bf16)
    padded = jnp.pad(activations, ((0, 0), (0, padded_rows - quarter_rows)))
    partial = lax.dot_general(
        padded, weighted, (((0,), (0,)), ((), ())), preferred_element_type=f32
    ).astype(bf16)
    width = partial.shape[1]

    steps = decode_hidden.shape[1]
    by_quarter = jnp.pad(
        decode_hidden.reshape(steps * TP, quarter_rows), ((0, 0), (0, padded_rows - quarter_rows))
    )
    blocks = NY * NZ
    lanes = NX * PAD
    spread = pick(
        padded_rows,
        blocks * lanes,
        lambda r, c: (r // (OWN * blocks) == c % lanes // PAD)
        & (r // OWN % blocks == c // lanes)
        & (r % OWN == c % PAD),
    )
    placed_h = jnp.dot(by_quarter, spread, preferred_element_type=f32).astype(bf16)
    placed_h = placed_h.reshape(steps * TP, blocks, lanes).transpose(1, 0, 2).reshape(blocks, width)

    got = lax.all_to_all(partial, "x", 0, 0, tiled=True)
    part_x = jnp.sum(got.reshape(NX, -1, width).astype(f32), axis=0).astype(bf16)
    stretch = pick(
        blocks * PAD,
        blocks * PAD,
        lambda r, c: jnp.where(
            c < blocks * OWN,
            (r // PAD == c // OWN) & (r % PAD == c % OWN),
            (r // PAD == c - blocks * OWN) & (r % PAD == OWN),
        ),
    )
    part_x = jnp.dot(
        stretch, jnp.concatenate([part_x, placed_h], axis=0), preferred_element_type=f32
    ).astype(bf16)
    got = lax.all_to_all(part_x, ("y", "z"), 0, 0, tiled=True).reshape(blocks, PAD, width)
    gradient = jnp.sum(got[:, :OWN].astype(f32), axis=0).reshape(key_master.shape)
    hidden_yz = got[:, OWN].reshape(blocks * steps, TP * lanes)

    corr_one = 1.0 - 0.9**10
    corr_two = 1.0 - 0.95**10
    moment_one_new = 0.9 * moment_one + 0.1 * gradient
    moment_two_new = 0.95 * moment_two + 0.05 * gradient * gradient
    master_new = key_master - 0.005 * (moment_one_new / corr_one) / (
        jnp.sqrt(moment_two_new / corr_two) + 1e-08
    )
    relay = jnp.pad(master_new[0].astype(bf16), ((0, PAD - OWN), (0, 0)))

    heads = relay.reshape(PAD, TP, HD).transpose(1, 0, 2)
    send = jnp.broadcast_to(heads[:, None], (TP, NX, PAD, HD)).reshape(-1, HD)
    weight = lax.all_to_all(send, ("h", "c", "x"), 0, 0, tiled=True)
    keys_yz = jnp.dot(hidden_yz, weight, preferred_element_type=f32)
    got = lax.all_to_all(keys_yz.reshape(blocks, steps, HD), ("y", "z"), 0, 0, tiled=True)
    new_keys = jnp.sum(got, axis=0).astype(bf16)[None]

    flat_hidden = decode_hidden.reshape(steps, -1)
    new_values = jnp.dot(flat_hidden, value_weight, preferred_element_type=f32).astype(bf16)[None]
    attention = attend(queries, cache_keys, cache_values, cache_len, new_keys, new_values)
    return (master_new, moment_one_new, moment_two_new, new_keys, new_values, attention)


def solution(mesh):
    grid = Mesh(mesh.devices.reshape(NX, NY, NZ, 2, 2), ("x", "y", "z", "h", "c"))
    grp, tp = ("x", "y", "z"), ("h", "c")
    placed = (
        P(grp, tp),
        P(grp, None),
        P(),
        P(),
        P(tp, grp, None),
        P(tp, grp, None),
        P(tp, grp, None),
        P(grp, None, None),
        P(grp, None, tp),
        P(grp, None, tp),
        P(grp, None, tp),
        P(grp),
        P(None, tp),
    )
    return jax.shard_map(
        shards,
        mesh=grid,
        in_specs=placed,
        out_specs=(
            P(tp, grp, None),
            P(tp, grp, None),
            P(tp, grp, None),
            P(grp, None, tp),
            P(grp, None, tp),
            P(grp, None, tp),
        ),
        check_vma=False,
    )
```

```python
import math

import jax
import jax.numpy as jnp
import numpy as np
from jax import lax
from jax.experimental import pallas as pl
from jax.experimental.pallas import tpu as pltpu
from jax.sharding import Mesh, PartitionSpec as P

HD = 128
GQA = 5
SEQ = 256
NX, NY, NZ = 4, 4, 12
OWN = 7
PAD = 8
TP = 4


def cache_scores(queries, cache_keys, cache_len):
    rows, steps, width = queries.shape
    length = cache_keys.shape[1]
    heads_kv = cache_keys.shape[2] // HD
    shaped_q = queries.reshape(rows, steps, heads_kv, GQA, HD)
    keys_c = cache_keys.reshape(rows, length, heads_kv, HD)
    score_c = jnp.einsum(
        "rsgqd,rcgd->rgsqc", shaped_q, keys_c, preferred_element_type=jnp.float32
    ) * (1.0 / math.sqrt(HD))
    valid = jnp.arange(length, dtype=jnp.int32)[None, :] < cache_len[:, None]
    score_c = jnp.where(valid[:, None, None, None, :], score_c, -jnp.inf)
    return shaped_q, score_c, jnp.max(score_c, axis=-1)


def attend(shaped_q, score_c, top_c, causal, cache_values, new_keys, new_values):
    rows, steps, heads_kv = shaped_q.shape[:3]
    length = cache_values.shape[1]
    inverse = 1.0 / math.sqrt(HD)
    vals_c = cache_values.reshape(rows, length, heads_kv, HD)
    keys_n = new_keys.reshape(rows, steps, heads_kv, HD)
    vals_n = new_values.reshape(rows, steps, heads_kv, HD)
    score_n = (
        jnp.einsum("rsgqd,rtgd->rgsqt", shaped_q, keys_n, preferred_element_type=jnp.float32)
        * inverse
    )
    score_n = jnp.where(causal[None, None, :, None, :], score_n, -jnp.inf)
    top = jnp.maximum(top_c, jnp.max(score_n, axis=-1))
    exp_c = jnp.exp(score_c - top[..., None])
    exp_n = jnp.exp(score_n - top[..., None])
    total = jnp.sum(exp_c, axis=-1) + jnp.sum(exp_n, axis=-1)
    probs_c = (exp_c / total[..., None]).astype(jnp.bfloat16)
    probs_n = (exp_n / total[..., None]).astype(jnp.bfloat16)
    mixed = jnp.einsum("rgsqc,rcgd->rsgqd", probs_c, vals_c, preferred_element_type=jnp.float32)
    mixed = mixed + jnp.einsum(
        "rgsqt,rtgd->rsgqd", probs_n, vals_n, preferred_element_type=jnp.float32
    )
    return mixed.astype(jnp.bfloat16).reshape(rows, steps, -1)


def pick(target, size):
    c = lax.broadcasted_iota(jnp.int32, (len(target), size), 1)
    return (jnp.asarray(target, jnp.int32)[:, None] == c).astype(jnp.bfloat16)


def gradient_kernel(len_ref, adv_ref, act_ref, cot_ref, out_ref, wgt_ref):
    tok_rows, quarter_rows = act_ref.shape
    group = lax.axis_index(("x", "y", "z"))
    length = len_ref[group]
    adv = adv_ref[group].astype(jnp.float32)
    within = lax.broadcasted_iota(jnp.int32, (tok_rows, HD), 0)
    scale = jnp.where(within < length, adv / 256.0, jnp.float32(0.0)) / len_ref.shape[0]
    for c in range(cot_ref.shape[1] // HD):
        cols = pl.ds(c * HD, HD)
        wgt_ref[:, cols] = (cot_ref[:, cols].astype(jnp.float32) * scale).astype(jnp.bfloat16)
    out_ref[:quarter_rows, :] = lax.dot_general(
        act_ref[...],
        wgt_ref[...],
        (((0,), (0,)), ((), ())),
        preferred_element_type=jnp.float32,
    ).astype(jnp.bfloat16)
    rest = out_ref.shape[0] - quarter_rows
    out_ref[quarter_rows:, :] = jnp.zeros((rest, out_ref.shape[1]), jnp.bfloat16)


def shards(
    activations,
    cotangent,
    advantage,
    seq_len,
    key_master,
    moment_one,
    moment_two,
    decode_hidden,
    queries,
    cache_keys,
    cache_values,
    cache_len,
    value_weight,
):
    bf16, f32 = jnp.bfloat16, jnp.float32
    tok_rows, quarter_rows = activations.shape
    padded_rows = OWN * NX * NY * NZ
    width = cotangent.shape[1]
    smem = pl.BlockSpec(memory_space=pltpu.SMEM)
    vmem = pl.BlockSpec(memory_space=pltpu.VMEM)
    partial = pl.pallas_call(
        gradient_kernel,
        out_shape=jax.ShapeDtypeStruct((padded_rows, width), bf16),
        in_specs=[smem, smem, vmem, vmem],
        out_specs=vmem,
        scratch_shapes=[pltpu.VMEM((tok_rows, width), bf16)],
        name="gradient",
    )(seq_len, advantage, activations, cotangent)

    steps = decode_hidden.shape[1]
    cores = TP // 2
    half = cores * quarter_rows
    mine = lax.dynamic_slice_in_dim(decode_hidden[0], lax.axis_index("h") * half, half, axis=1)
    by_quarter = jnp.pad(
        mine.reshape(steps * cores, quarter_rows), ((0, 0), (0, padded_rows - quarter_rows))
    )
    blocks = NY * NZ
    lanes = NX * PAD
    r = np.arange(padded_rows)
    spread = pick(
        r // OWN % blocks * lanes + r // (OWN * blocks) * PAD + r % OWN, blocks * lanes
    )
    placed_h = jnp.dot(by_quarter, spread, preferred_element_type=f32).astype(bf16)
    used = steps * cores * lanes
    placed_h = placed_h.reshape(steps * cores, blocks, lanes).transpose(1, 0, 2)
    placed_h = jnp.pad(placed_h.reshape(blocks, used), ((0, 0), (0, width - used)))

    r, q = np.arange(blocks * OWN), np.arange(blocks)
    stretch = pick(r // OWN * PAD + r % OWN, blocks * PAD)
    lasts = jnp.dot(
        pick(q * PAD + OWN, blocks * PAD).T, placed_h, preferred_element_type=f32
    ).astype(bf16)

    got = lax.all_to_all(partial, "x", 0, 0, tiled=True)
    part_x = jnp.sum(got.reshape(NX, -1, width).astype(f32), axis=0).astype(bf16)
    part_x = (jnp.dot(stretch.T, part_x, preferred_element_type=f32) + lasts).astype(bf16)
    got = lax.all_to_all(part_x, ("y", "z"), 0, 0, tiled=True).reshape(blocks, PAD, width)
    gradient = jnp.sum(got[:, :OWN].astype(f32), axis=0).reshape(key_master.shape)
    hidden_yz = got[:, OWN, :used].reshape(blocks * steps, cores * lanes)

    corr_one = 1.0 - 0.9**10
    corr_two = 1.0 - 0.95**10
    moment_one_new = 0.9 * moment_one + 0.1 * gradient
    moment_two_new = 0.95 * moment_two + 0.05 * gradient * gradient
    master_new = key_master - 0.005 * (moment_one_new / corr_one) / (
        jnp.sqrt(moment_two_new / corr_two) + 1e-08
    )
    relay = jnp.pad(master_new[0].astype(bf16), ((0, PAD - OWN), (0, 0)))

    heads = relay.reshape(PAD, 2, cores, HD).transpose(2, 0, 1, 3).reshape(cores, PAD, 2 * HD)
    send = jnp.broadcast_to(heads[:, None], (cores, NX, PAD, 2 * HD)).reshape(-1, 2 * HD)
    weight = lax.all_to_all(send, ("c", "x"), 0, 0, tiled=True)
    keys = jnp.stack(
        [jnp.dot(hidden_yz, weight[:, h * HD : (h + 1) * HD], preferred_element_type=f32) for h in range(2)]
    )
    got = lax.all_to_all(keys.reshape(-1, steps, HD), ("h", "y", "z"), 0, 0, tiled=True)
    new_keys = jnp.sum(got, axis=0).astype(bf16)[None]

    flat_hidden = decode_hidden.reshape(steps, -1)
    new_values = jnp.dot(flat_hidden, value_weight, preferred_element_type=f32).astype(bf16)[None]
    shaped_q, score_c, top_c = cache_scores(queries, cache_keys, cache_len)
    causal = (
        jnp.arange(steps, dtype=jnp.int32)[None, :] <= jnp.arange(steps, dtype=jnp.int32)[:, None]
    )
    attention = attend(shaped_q, score_c, top_c, causal, cache_values, new_keys, new_values)
    return (master_new, moment_one_new, moment_two_new, new_keys, new_values, attention)


def solution(mesh):
    grid = Mesh(mesh.devices.reshape(NX, NY, NZ, 2, 2), ("x", "y", "z", "h", "c"))
    grp, tp = ("x", "y", "z"), ("h", "c")
    placed = (
        P(grp, tp),
        P(grp, None),
        P(),
        P(),
        P(tp, grp, None),
        P(tp, grp, None),
        P(tp, grp, None),
        P(grp, None, None),
        P(grp, None, tp),
        P(grp, None, tp),
        P(grp, None, tp),
        P(grp),
        P(None, tp),
    )
    return jax.shard_map(
        shards,
        mesh=grid,
        in_specs=placed,
        out_specs=(
            P(tp, grp, None),
            P(tp, grp, None),
            P(tp, grp, None),
            P(grp, None, tp),
            P(grp, None, tp),
            P(grp, None, tp),
        ),
        check_vma=False,
    )
```

```python
import math

import jax
import jax.numpy as jnp
import numpy as np
from jax import lax
from jax.experimental import pallas as pl
from jax.experimental.pallas import tpu as pltpu
from jax.sharding import Mesh, PartitionSpec as P

HD = 128
GQA = 5
SEQ = 256
NX, NY, NZ = 4, 4, 12
OWN = 7
PAD = 8
TP = 4


def cache_scores(queries, cache_keys, cache_len):
    rows, steps, width = queries.shape
    length = cache_keys.shape[1]
    heads_kv = cache_keys.shape[2] // HD
    shaped_q = queries.reshape(rows, steps, heads_kv, GQA, HD)
    keys_c = cache_keys.reshape(rows, length, heads_kv, HD)
    score_c = jnp.einsum(
        "rsgqd,rcgd->rgsqc", shaped_q, keys_c, preferred_element_type=jnp.float32
    ) * (1.0 / math.sqrt(HD))
    valid = jnp.arange(length, dtype=jnp.int32)[None, :] < cache_len[:, None]
    score_c = jnp.where(valid[:, None, None, None, :], score_c, -jnp.inf)
    return shaped_q, score_c, jnp.max(score_c, axis=-1)


def attend(shaped_q, score_c, top_c, causal, cache_values, new_keys, new_values):
    rows, steps, heads_kv = shaped_q.shape[:3]
    length = cache_values.shape[1]
    inverse = 1.0 / math.sqrt(HD)
    vals_c = cache_values.reshape(rows, length, heads_kv, HD)
    keys_n = new_keys.reshape(rows, steps, heads_kv, HD)
    vals_n = new_values.reshape(rows, steps, heads_kv, HD)
    score_n = (
        jnp.einsum("rsgqd,rtgd->rgsqt", shaped_q, keys_n, preferred_element_type=jnp.float32)
        * inverse
    )
    score_n = jnp.where(causal[None, None, :, None, :], score_n, -jnp.inf)
    top = jnp.maximum(top_c, jnp.max(score_n, axis=-1))
    exp_c = jnp.exp(score_c - top[..., None])
    exp_n = jnp.exp(score_n - top[..., None])
    total = jnp.sum(exp_c, axis=-1) + jnp.sum(exp_n, axis=-1)
    probs_c = (exp_c / total[..., None]).astype(jnp.bfloat16)
    probs_n = (exp_n / total[..., None]).astype(jnp.bfloat16)
    mixed = jnp.einsum("rgsqc,rcgd->rsgqd", probs_c, vals_c, preferred_element_type=jnp.float32)
    mixed = mixed + jnp.einsum(
        "rgsqt,rtgd->rsgqd", probs_n, vals_n, preferred_element_type=jnp.float32
    )
    return mixed.astype(jnp.bfloat16).reshape(rows, steps, -1)


def pick(target, size):
    c = lax.broadcasted_iota(jnp.int32, (len(target), size), 1)
    return (jnp.asarray(target, jnp.int32)[:, None] == c).astype(jnp.bfloat16)


def gradient_kernel(len_ref, adv_ref, act_ref, cot_ref, out_ref, wgt_ref):
    tok_rows, quarter_rows = act_ref.shape
    group = lax.axis_index(("x", "y", "z"))
    length = len_ref[group]
    adv = adv_ref[group].astype(jnp.float32)
    within = lax.broadcasted_iota(jnp.int32, (tok_rows, HD), 0)
    scale = jnp.where(within < length, adv / 256.0, jnp.float32(0.0)) / len_ref.shape[0]
    for c in range(cot_ref.shape[1] // HD):
        cols = pl.ds(c * HD, HD)
        wgt_ref[:, cols] = (cot_ref[:, cols].astype(jnp.float32) * scale).astype(jnp.bfloat16)
    out_ref[:quarter_rows, :] = lax.dot_general(
        act_ref[...],
        wgt_ref[...],
        (((0,), (0,)), ((), ())),
        preferred_element_type=jnp.float32,
    ).astype(jnp.bfloat16)
    rest = out_ref.shape[0] - quarter_rows
    out_ref[quarter_rows:, :] = jnp.zeros((rest, out_ref.shape[1]), jnp.bfloat16)


def blocks_kernel(got_ref, hidden_ref, out_ref):
    total = got_ref[0].astype(jnp.float32)
    for i in range(1, NX):
        total = total + got_ref[i].astype(jnp.float32)
    rows, own = out_ref.shape[0], got_ref.shape[1]
    r = lax.broadcasted_iota(jnp.int32, (rows, own), 0)
    c = lax.broadcasted_iota(jnp.int32, (rows, own), 1)
    keep = ((r // PAD) * OWN + r % PAD == c) & (r % PAD < OWN)
    body = jnp.dot(
        keep.astype(jnp.bfloat16), total.astype(jnp.bfloat16), preferred_element_type=jnp.float32
    )
    count = hidden_ref.shape[0]
    r = lax.broadcasted_iota(jnp.int32, (rows, count), 0)
    c = lax.broadcasted_iota(jnp.int32, (rows, count), 1)
    last = r == c * PAD + OWN
    body = body + jnp.dot(
        last.astype(jnp.bfloat16), hidden_ref[...], preferred_element_type=jnp.float32
    )
    out_ref[...] = body.astype(jnp.bfloat16)


def shards(
    activations,
    cotangent,
    advantage,
    seq_len,
    key_master,
    moment_one,
    moment_two,
    decode_hidden,
    queries,
    cache_keys,
    cache_values,
    cache_len,
    value_weight,
):
    bf16, f32 = jnp.bfloat16, jnp.float32
    tok_rows, quarter_rows = activations.shape
    padded_rows = OWN * NX * NY * NZ
    width = cotangent.shape[1]
    smem = pl.BlockSpec(memory_space=pltpu.SMEM)
    vmem = pl.BlockSpec(memory_space=pltpu.VMEM)
    small = pltpu.CompilerParams(vmem_limit_bytes=16 * 2**20)
    partial = pl.pallas_call(
        gradient_kernel,
        out_shape=jax.ShapeDtypeStruct((padded_rows, width), bf16),
        in_specs=[smem, smem, vmem, vmem],
        out_specs=vmem,
        scratch_shapes=[pltpu.VMEM((tok_rows, width), bf16)],
        name="gradient",
    )(seq_len, advantage, activations, cotangent)

    steps = decode_hidden.shape[1]
    by_quarter = jnp.pad(
        decode_hidden.reshape(steps * TP, quarter_rows), ((0, 0), (0, padded_rows - quarter_rows))
    )
    blocks = NY * NZ
    lanes = NX * PAD
    r = np.arange(padded_rows)
    spread = pick(
        r // OWN % blocks * lanes + r // (OWN * blocks) * PAD + r % OWN, blocks * lanes
    )
    placed_h = jnp.dot(by_quarter, spread, preferred_element_type=f32).astype(bf16)
    placed_h = placed_h.reshape(steps * TP, blocks, lanes).transpose(1, 0, 2).reshape(blocks, width)

    got = lax.all_to_all(partial, "x", 0, 0, tiled=True)
    part_x = pl.pallas_call(
        blocks_kernel,
        out_shape=jax.ShapeDtypeStruct((blocks * PAD, width), bf16),
        in_specs=[vmem, vmem],
        out_specs=vmem,
        compiler_params=small,
        name="blocks",
    )(got.reshape(NX, blocks * OWN, width), placed_h)
    got = lax.all_to_all(part_x, ("y", "z"), 0, 0, tiled=True).reshape(blocks, PAD, width)
    gradient = jnp.sum(got[:, :OWN].astype(f32), axis=0).reshape(key_master.shape)
    hidden_yz = got[:, OWN].reshape(blocks * steps, TP * lanes)

    corr_one = 1.0 - 0.9**10
    corr_two = 1.0 - 0.95**10
    moment_one_new = 0.9 * moment_one + 0.1 * gradient
    moment_two_new = 0.95 * moment_two + 0.05 * gradient * gradient
    master_new = key_master - 0.005 * (moment_one_new / corr_one) / (
        jnp.sqrt(moment_two_new / corr_two) + 1e-08
    )
    relay = jnp.pad(master_new[0].astype(bf16), ((0, PAD - OWN), (0, 0)))

    heads = relay.reshape(PAD, TP, HD).transpose(1, 0, 2)
    send = jnp.broadcast_to(heads[:, None], (TP, NX, PAD, HD)).reshape(-1, HD)
    flat_hidden = decode_hidden.reshape(steps, -1)
    new_values = jnp.dot(flat_hidden, value_weight, preferred_element_type=f32).astype(bf16)[None]
    shaped_q, score_c, top_c = cache_scores(queries, cache_keys, cache_len)
    causal = (
        jnp.arange(steps, dtype=jnp.int32)[None, :] <= jnp.arange(steps, dtype=jnp.int32)[:, None]
    )
    send, hidden_yz, new_values, score_c, top_c, causal = lax.optimization_barrier(
        (send, hidden_yz, new_values, score_c, top_c, causal)
    )
    weight = lax.all_to_all(send, ("h", "c", "x"), 0, 0, tiled=True)
    keys_yz = jnp.dot(hidden_yz, weight, preferred_element_type=f32)
    got = lax.all_to_all(keys_yz.reshape(blocks, steps, HD), ("y", "z"), 0, 0, tiled=True)
    new_keys = jnp.sum(got, axis=0).astype(bf16)[None]

    attention = attend(shaped_q, score_c, top_c, causal, cache_values, new_keys, new_values)
    return (master_new, moment_one_new, moment_two_new, new_keys, new_values, attention)


def solution(mesh):
    grid = Mesh(mesh.devices.reshape(NX, NY, NZ, 2, 2), ("x", "y", "z", "h", "c"))
    grp, tp = ("x", "y", "z"), ("h", "c")
    placed = (
        P(grp, tp),
        P(grp, None),
        P(),
        P(),
        P(tp, grp, None),
        P(tp, grp, None),
        P(tp, grp, None),
        P(grp, None, None),
        P(grp, None, tp),
        P(grp, None, tp),
        P(grp, None, tp),
        P(grp),
        P(None, tp),
    )
    return jax.shard_map(
        shards,
        mesh=grid,
        in_specs=placed,
        out_specs=(
            P(tp, grp, None),
            P(tp, grp, None),
            P(tp, grp, None),
            P(grp, None, tp),
            P(grp, None, tp),
            P(grp, None, tp),
        ),
        check_vma=False,
    )
```

```python
import math

import jax
import jax.numpy as jnp
import numpy as np
from jax import lax
from jax.experimental import pallas as pl
from jax.experimental.pallas import tpu as pltpu
from jax.sharding import Mesh, PartitionSpec as P

HD = 128
GQA = 5
SEQ = 256
NX, NY, NZ = 4, 4, 12
OWN = 7
PAD = 8
TP = 4


def cache_scores(queries, cache_keys, cache_len):
    rows, steps, width = queries.shape
    length = cache_keys.shape[1]
    heads_kv = cache_keys.shape[2] // HD
    shaped_q = queries.reshape(rows, steps, heads_kv, GQA, HD)
    keys_c = cache_keys.reshape(rows, length, heads_kv, HD)
    score_c = jnp.einsum(
        "rsgqd,rcgd->rgsqc", shaped_q, keys_c, preferred_element_type=jnp.float32
    ) * (1.0 / math.sqrt(HD))
    valid = jnp.arange(length, dtype=jnp.int32)[None, :] < cache_len[:, None]
    score_c = jnp.where(valid[:, None, None, None, :], score_c, -jnp.inf)
    return shaped_q, score_c, jnp.max(score_c, axis=-1)


def attend(shaped_q, score_c, top_c, causal, cache_values, new_keys, new_values):
    rows, steps, heads_kv = shaped_q.shape[:3]
    length = cache_values.shape[1]
    inverse = 1.0 / math.sqrt(HD)
    vals_c = cache_values.reshape(rows, length, heads_kv, HD)
    keys_n = new_keys.reshape(rows, steps, heads_kv, HD)
    vals_n = new_values.reshape(rows, steps, heads_kv, HD)
    score_n = (
        jnp.einsum("rsgqd,rtgd->rgsqt", shaped_q, keys_n, preferred_element_type=jnp.float32)
        * inverse
    )
    score_n = jnp.where(causal[None, None, :, None, :], score_n, -jnp.inf)
    top = jnp.maximum(top_c, jnp.max(score_n, axis=-1))
    exp_c = jnp.exp(score_c - top[..., None])
    exp_n = jnp.exp(score_n - top[..., None])
    total = jnp.sum(exp_c, axis=-1) + jnp.sum(exp_n, axis=-1)
    probs_c = (exp_c / total[..., None]).astype(jnp.bfloat16)
    probs_n = (exp_n / total[..., None]).astype(jnp.bfloat16)
    mixed = jnp.einsum("rgsqc,rcgd->rsgqd", probs_c, vals_c, preferred_element_type=jnp.float32)
    mixed = mixed + jnp.einsum(
        "rgsqt,rtgd->rsgqd", probs_n, vals_n, preferred_element_type=jnp.float32
    )
    return mixed.astype(jnp.bfloat16).reshape(rows, steps, -1)


def pick(target, size):
    c = lax.broadcasted_iota(jnp.int32, (len(target), size), 1)
    return (jnp.asarray(target, jnp.int32)[:, None] == c).astype(jnp.bfloat16)


def gradient_kernel(len_ref, adv_ref, act_ref, cot_ref, out_ref, wgt_ref):
    tok_rows, quarter_rows = act_ref.shape
    group = lax.axis_index(("x", "y", "z"))
    length = len_ref[group]
    adv = adv_ref[group].astype(jnp.float32)
    within = lax.broadcasted_iota(jnp.int32, (tok_rows, HD), 0)
    scale = jnp.where(within < length, adv / 256.0, jnp.float32(0.0)) / len_ref.shape[0]
    for c in range(cot_ref.shape[1] // HD):
        cols = pl.ds(c * HD, HD)
        wgt_ref[:, cols] = (cot_ref[:, cols].astype(jnp.float32) * scale).astype(jnp.bfloat16)
    out_ref[:quarter_rows, :] = lax.dot_general(
        act_ref[...],
        wgt_ref[...],
        (((0,), (0,)), ((), ())),
        preferred_element_type=jnp.float32,
    ).astype(jnp.bfloat16)
    rest = out_ref.shape[0] - quarter_rows
    out_ref[quarter_rows:, :] = jnp.zeros((rest, out_ref.shape[1]), jnp.bfloat16)


def blocks_kernel(got_ref, hidden_ref, out_ref):
    total = got_ref[0].astype(jnp.float32)
    for i in range(1, NX):
        total = total + got_ref[i].astype(jnp.float32)
    rows, own = out_ref.shape[0], got_ref.shape[1]
    r = lax.broadcasted_iota(jnp.int32, (rows, own), 0)
    c = lax.broadcasted_iota(jnp.int32, (rows, own), 1)
    block = r // PAD
    keep = ((block % NY * NZ + block // NY) * OWN + r % PAD == c) & (r % PAD < OWN)
    body = jnp.dot(
        keep.astype(jnp.bfloat16), total.astype(jnp.bfloat16), preferred_element_type=jnp.float32
    )
    count = hidden_ref.shape[0]
    r = lax.broadcasted_iota(jnp.int32, (rows, count), 0)
    c = lax.broadcasted_iota(jnp.int32, (rows, count), 1)
    last = r == c * PAD + OWN
    body = body + jnp.dot(
        last.astype(jnp.bfloat16), hidden_ref[...], preferred_element_type=jnp.float32
    )
    out_ref[...] = body.astype(jnp.bfloat16)


def shards(
    activations,
    cotangent,
    advantage,
    seq_len,
    key_master,
    moment_one,
    moment_two,
    decode_hidden,
    queries,
    cache_keys,
    cache_values,
    cache_len,
    value_weight,
):
    bf16, f32 = jnp.bfloat16, jnp.float32
    tok_rows, quarter_rows = activations.shape
    padded_rows = OWN * NX * NY * NZ
    width = cotangent.shape[1]
    smem = pl.BlockSpec(memory_space=pltpu.SMEM)
    vmem = pl.BlockSpec(memory_space=pltpu.VMEM)
    small = pltpu.CompilerParams(vmem_limit_bytes=16 * 2**20)
    partial = pl.pallas_call(
        gradient_kernel,
        out_shape=jax.ShapeDtypeStruct((padded_rows, width), bf16),
        in_specs=[smem, smem, vmem, vmem],
        out_specs=vmem,
        scratch_shapes=[pltpu.VMEM((tok_rows, width), bf16)],
        name="gradient",
    )(seq_len, advantage, activations, cotangent)

    steps = decode_hidden.shape[1]
    by_quarter = jnp.pad(
        decode_hidden.reshape(steps * TP, quarter_rows), ((0, 0), (0, padded_rows - quarter_rows))
    )
    blocks = NY * NZ
    lanes = NX * PAD
    r = np.arange(padded_rows)
    block = r // OWN % NZ * NY + r // (OWN * NZ) % NY
    spread = pick(
        block * lanes + r // (OWN * blocks) * PAD + r % OWN, blocks * lanes
    )
    placed_h = jnp.dot(by_quarter, spread, preferred_element_type=f32).astype(bf16)
    placed_h = placed_h.reshape(steps * TP, blocks, lanes).transpose(1, 0, 2).reshape(blocks, width)

    got = lax.all_to_all(partial, "x", 0, 0, tiled=True)
    flat_hidden = decode_hidden.reshape(steps, -1)
    new_values = jnp.dot(flat_hidden, value_weight, preferred_element_type=f32).astype(bf16)[None]
    shaped_q, score_c, top_c = cache_scores(queries, cache_keys, cache_len)
    causal = (
        jnp.arange(steps, dtype=jnp.int32)[None, :] <= jnp.arange(steps, dtype=jnp.int32)[:, None]
    )
    got, placed_h, new_values, score_c, top_c, causal = lax.optimization_barrier(
        (got, placed_h, new_values, score_c, top_c, causal)
    )
    part_x = pl.pallas_call(
        blocks_kernel,
        out_shape=jax.ShapeDtypeStruct((blocks * PAD, width), bf16),
        in_specs=[vmem, vmem],
        out_specs=vmem,
        compiler_params=small,
        name="blocks",
    )(got.reshape(NX, blocks * OWN, width), placed_h)
    got = lax.all_to_all(part_x, ("z", "y"), 0, 0, tiled=True).reshape(blocks, PAD, width)
    gradient = jnp.sum(got[:, :OWN].astype(f32), axis=0).reshape(key_master.shape)
    hidden_yz = got[:, OWN].reshape(blocks * steps, TP * lanes)

    corr_one = 1.0 - 0.9**10
    corr_two = 1.0 - 0.95**10
    moment_one_new = 0.9 * moment_one + 0.1 * gradient
    moment_two_new = 0.95 * moment_two + 0.05 * gradient * gradient
    master_new = key_master - 0.005 * (moment_one_new / corr_one) / (
        jnp.sqrt(moment_two_new / corr_two) + 1e-08
    )
    relay = jnp.pad(master_new[0].astype(bf16), ((0, PAD - OWN), (0, 0)))

    heads = relay.reshape(PAD, TP, HD).transpose(1, 0, 2)
    send = jnp.broadcast_to(heads[:, None], (TP, NX, PAD, HD)).reshape(-1, HD)
    send, hidden_yz = lax.optimization_barrier((send, hidden_yz))
    weight = lax.all_to_all(send, ("h", "c", "x"), 0, 0, tiled=True)
    keys_yz = jnp.dot(hidden_yz, weight, preferred_element_type=f32)
    got = lax.all_to_all(keys_yz.reshape(blocks, steps, HD), ("z", "y"), 0, 0, tiled=True)
    new_keys = jnp.sum(got, axis=0).astype(bf16)[None]

    attention = attend(shaped_q, score_c, top_c, causal, cache_values, new_keys, new_values)
    return (master_new, moment_one_new, moment_two_new, new_keys, new_values, attention)


def solution(mesh):
    grid = Mesh(mesh.devices.reshape(NX, NY, NZ, 2, 2), ("x", "y", "z", "h", "c"))
    grp, tp = ("x", "y", "z"), ("h", "c")
    placed = (
        P(grp, tp),
        P(grp, None),
        P(),
        P(),
        P(tp, grp, None),
        P(tp, grp, None),
        P(tp, grp, None),
        P(grp, None, None),
        P(grp, None, tp),
        P(grp, None, tp),
        P(grp, None, tp),
        P(grp),
        P(None, tp),
    )
    return jax.shard_map(
        shards,
        mesh=grid,
        in_specs=placed,
        out_specs=(
            P(tp, grp, None),
            P(tp, grp, None),
            P(tp, grp, None),
            P(grp, None, tp),
            P(grp, None, tp),
            P(grp, None, tp),
        ),
        check_vma=False,
    )
```

```python
import math

import jax
import jax.numpy as jnp
import numpy as np
from jax import lax
from jax.experimental import pallas as pl
from jax.experimental.pallas import tpu as pltpu
from jax.sharding import Mesh, PartitionSpec as P

HD = 128
GQA = 5
SEQ = 256
NX, NY, NZ = 4, 4, 12
OWN = 7
PAD = 8
TP = 4
CHUNK = 256


def cache_scores(queries, cache_keys, cache_len):
    rows, steps, width = queries.shape
    length = cache_keys.shape[1]
    heads_kv = cache_keys.shape[2] // HD
    shaped_q = queries.reshape(rows, steps, heads_kv, GQA, HD)
    keys_c = cache_keys.reshape(rows, length, heads_kv, HD)
    score_c = jnp.einsum(
        "rsgqd,rcgd->rgsqc", shaped_q, keys_c, preferred_element_type=jnp.float32
    ) * (1.0 / math.sqrt(HD))
    valid = jnp.arange(length, dtype=jnp.int32)[None, :] < cache_len[:, None]
    score_c = jnp.where(valid[:, None, None, None, :], score_c, -jnp.inf)
    return shaped_q, score_c, jnp.max(score_c, axis=-1)


def attend(shaped_q, score_c, top_c, causal, cache_values, new_keys, new_values):
    rows, steps, heads_kv = shaped_q.shape[:3]
    length = cache_values.shape[1]
    inverse = 1.0 / math.sqrt(HD)
    vals_c = cache_values.reshape(rows, length, heads_kv, HD)
    keys_n = new_keys.reshape(rows, steps, heads_kv, HD)
    vals_n = new_values.reshape(rows, steps, heads_kv, HD)
    score_n = (
        jnp.einsum("rsgqd,rtgd->rgsqt", shaped_q, keys_n, preferred_element_type=jnp.float32)
        * inverse
    )
    score_n = jnp.where(causal[None, None, :, None, :], score_n, -jnp.inf)
    top = jnp.maximum(top_c, jnp.max(score_n, axis=-1))
    exp_c = jnp.exp(score_c - top[..., None])
    exp_n = jnp.exp(score_n - top[..., None])
    total = jnp.sum(exp_c, axis=-1) + jnp.sum(exp_n, axis=-1)
    probs_c = (exp_c / total[..., None]).astype(jnp.bfloat16)
    probs_n = (exp_n / total[..., None]).astype(jnp.bfloat16)
    mixed = jnp.einsum("rgsqc,rcgd->rsgqd", probs_c, vals_c, preferred_element_type=jnp.float32)
    mixed = mixed + jnp.einsum(
        "rgsqt,rtgd->rsgqd", probs_n, vals_n, preferred_element_type=jnp.float32
    )
    return mixed.astype(jnp.bfloat16).reshape(rows, steps, -1)


def pick(target, size):
    c = lax.broadcasted_iota(jnp.int32, (len(target), size), 1)
    return (jnp.asarray(target, jnp.int32)[:, None] == c).astype(jnp.bfloat16)


def gradient_kernel(
    len_ref, adv_ref, act_hbm, cot_hbm, out_hbm, act_ref, cot_ref, wgt_ref, out_ref, sem
):
    tok_rows, quarter_rows = act_ref.shape
    parts = quarter_rows // CHUNK
    cot_in = pltpu.make_async_copy(cot_hbm, cot_ref, sem.at[0])
    cot_in.start()
    loads, stores = [], []
    for i in range(parts):
        cols = pl.ds(i * CHUNK, CHUNK)
        loads.append(
            pltpu.make_async_copy(act_hbm.at[:, cols], act_ref.at[:, cols], sem.at[1 + i])
        )
        loads[i].start()
        end = (i + 1) * CHUNK if i + 1 < parts else out_ref.shape[0]
        rows = pl.ds(i * CHUNK, end - i * CHUNK)
        stores.append(
            pltpu.make_async_copy(out_ref.at[rows], out_hbm.at[rows], sem.at[1 + parts + i])
        )
    rest = out_ref.shape[0] - quarter_rows
    out_ref[quarter_rows:, :] = jnp.zeros((rest, out_ref.shape[1]), jnp.bfloat16)
    group = lax.axis_index(("x", "y", "z"))
    length = len_ref[group]
    adv = adv_ref[group].astype(jnp.float32)
    within = lax.broadcasted_iota(jnp.int32, (tok_rows, HD), 0)
    scale = jnp.where(within < length, adv / 256.0, jnp.float32(0.0)) / len_ref.shape[0]
    cot_in.wait()
    for c in range(cot_ref.shape[1] // HD):
        cols = pl.ds(c * HD, HD)
        wgt_ref[:, cols] = (cot_ref[:, cols].astype(jnp.float32) * scale).astype(jnp.bfloat16)
    for i in range(parts):
        loads[i].wait()
        out_ref[i * CHUNK : (i + 1) * CHUNK, :] = lax.dot_general(
            act_ref[:, i * CHUNK : (i + 1) * CHUNK],
            wgt_ref[...],
            (((0,), (0,)), ((), ())),
            preferred_element_type=jnp.float32,
        ).astype(jnp.bfloat16)
        stores[i].start()
    for i in range(parts):
        stores[i].wait()


def blocks_kernel(got_ref, hidden_ref, out_ref):
    total = got_ref[0].astype(jnp.float32)
    for i in range(1, NX):
        total = total + got_ref[i].astype(jnp.float32)
    rows, own = out_ref.shape[0], got_ref.shape[1]
    r = lax.broadcasted_iota(jnp.int32, (rows, own), 0)
    c = lax.broadcasted_iota(jnp.int32, (rows, own), 1)
    block = r // PAD
    keep = ((block % NY * NZ + block // NY) * OWN + r % PAD == c) & (r % PAD < OWN)
    body = jnp.dot(
        keep.astype(jnp.bfloat16), total.astype(jnp.bfloat16), preferred_element_type=jnp.float32
    )
    count = hidden_ref.shape[0]
    r = lax.broadcasted_iota(jnp.int32, (rows, count), 0)
    c = lax.broadcasted_iota(jnp.int32, (rows, count), 1)
    last = r == c * PAD + OWN
    body = body + jnp.dot(
        last.astype(jnp.bfloat16), hidden_ref[...], preferred_element_type=jnp.float32
    )
    out_ref[...] = body.astype(jnp.bfloat16)


def shards(
    activations,
    cotangent,
    advantage,
    seq_len,
    key_master,
    moment_one,
    moment_two,
    decode_hidden,
    queries,
    cache_keys,
    cache_values,
    cache_len,
    value_weight,
):
    bf16, f32 = jnp.bfloat16, jnp.float32
    tok_rows, quarter_rows = activations.shape
    padded_rows = OWN * NX * NY * NZ
    width = cotangent.shape[1]
    smem = pl.BlockSpec(memory_space=pltpu.SMEM)
    vmem = pl.BlockSpec(memory_space=pltpu.VMEM)
    hbm = pl.BlockSpec(memory_space=pl.ANY)
    small = pltpu.CompilerParams(vmem_limit_bytes=16 * 2**20)
    partial = pl.pallas_call(
        gradient_kernel,
        out_shape=jax.ShapeDtypeStruct((padded_rows, width), bf16),
        in_specs=[smem, smem, hbm, hbm],
        out_specs=hbm,
        scratch_shapes=[
            pltpu.VMEM((tok_rows, quarter_rows), bf16),
            pltpu.VMEM((tok_rows, width), bf16),
            pltpu.VMEM((tok_rows, width), bf16),
            pltpu.VMEM((padded_rows, width), bf16),
            pltpu.SemaphoreType.DMA((1 + 2 * (quarter_rows // CHUNK),)),
        ],
        name="gradient",
    )(seq_len, advantage, activations, cotangent)

    steps = decode_hidden.shape[1]
    by_quarter = jnp.pad(
        decode_hidden.reshape(steps * TP, quarter_rows), ((0, 0), (0, padded_rows - quarter_rows))
    )
    blocks = NY * NZ
    lanes = NX * PAD
    r = np.arange(padded_rows)
    block = r // OWN % NZ * NY + r // (OWN * NZ) % NY
    spread = pick(
        block * lanes + r // (OWN * blocks) * PAD + r % OWN, blocks * lanes
    )
    placed_h = jnp.dot(by_quarter, spread, preferred_element_type=f32).astype(bf16)
    placed_h = placed_h.reshape(steps * TP, blocks, lanes).transpose(1, 0, 2).reshape(blocks, width)

    got = lax.all_to_all(partial, "x", 0, 0, tiled=True)
    flat_hidden = decode_hidden.reshape(steps, -1)
    new_values = jnp.dot(flat_hidden, value_weight, preferred_element_type=f32).astype(bf16)[None]
    shaped_q, score_c, top_c = cache_scores(queries, cache_keys, cache_len)
    causal = (
        jnp.arange(steps, dtype=jnp.int32)[None, :] <= jnp.arange(steps, dtype=jnp.int32)[:, None]
    )
    got, placed_h, new_values, score_c, top_c, causal = lax.optimization_barrier(
        (got, placed_h, new_values, score_c, top_c, causal)
    )
    part_x = pl.pallas_call(
        blocks_kernel,
        out_shape=jax.ShapeDtypeStruct((blocks * PAD, width), bf16),
        in_specs=[vmem, vmem],
        out_specs=vmem,
        compiler_params=small,
        name="blocks",
    )(got.reshape(NX, blocks * OWN, width), placed_h)
    got = lax.all_to_all(part_x, ("z", "y"), 0, 0, tiled=True).reshape(blocks, PAD, width)
    gradient = jnp.sum(got[:, :OWN].astype(f32), axis=0).reshape(key_master.shape)
    hidden_yz = got[:, OWN].reshape(blocks * steps, TP * lanes)

    corr_one = 1.0 - 0.9**10
    corr_two = 1.0 - 0.95**10
    moment_one_new = 0.9 * moment_one + 0.1 * gradient
    moment_two_new = 0.95 * moment_two + 0.05 * gradient * gradient
    master_new = key_master - 0.005 * (moment_one_new / corr_one) / (
        jnp.sqrt(moment_two_new / corr_two) + 1e-08
    )
    relay = jnp.pad(master_new[0].astype(bf16), ((0, PAD - OWN), (0, 0)))

    heads = relay.reshape(PAD, TP, HD).transpose(1, 0, 2)
    send = jnp.broadcast_to(heads[:, None], (TP, NX, PAD, HD)).reshape(-1, HD)
    send, hidden_yz = lax.optimization_barrier((send, hidden_yz))
    weight = lax.all_to_all(send, ("h", "c", "x"), 0, 0, tiled=True)
    keys_yz = jnp.dot(hidden_yz, weight, preferred_element_type=f32)
    got = lax.all_to_all(keys_yz.reshape(blocks, steps, HD), ("z", "y"), 0, 0, tiled=True)
    new_keys = jnp.sum(got, axis=0).astype(bf16)[None]

    attention = attend(shaped_q, score_c, top_c, causal, cache_values, new_keys, new_values)
    return (master_new, moment_one_new, moment_two_new, new_keys, new_values, attention)


def solution(mesh):
    grid = Mesh(mesh.devices.reshape(NX, NY, NZ, 2, 2), ("x", "y", "z", "h", "c"))
    grp, tp = ("x", "y", "z"), ("h", "c")
    placed = (
        P(grp, tp),
        P(grp, None),
        P(),
        P(),
        P(tp, grp, None),
        P(tp, grp, None),
        P(tp, grp, None),
        P(grp, None, None),
        P(grp, None, tp),
        P(grp, None, tp),
        P(grp, None, tp),
        P(grp),
        P(None, tp),
    )
    return jax.shard_map(
        shards,
        mesh=grid,
        in_specs=placed,
        out_specs=(
            P(tp, grp, None),
            P(tp, grp, None),
            P(tp, grp, None),
            P(grp, None, tp),
            P(grp, None, tp),
            P(grp, None, tp),
        ),
        check_vma=False,
    )
```

```python
import math

import jax
import jax.numpy as jnp
import numpy as np
from jax import lax
from jax.experimental import pallas as pl
from jax.experimental.pallas import tpu as pltpu
from jax.sharding import Mesh, PartitionSpec as P

HD = 128
GQA = 5
SEQ = 256
NX, NY, NZ = 4, 4, 12
OWN = 7
PAD = 8
TP = 4
CHUNK = 256


def cache_scores(queries, cache_keys, cache_len):
    rows, steps, width = queries.shape
    length = cache_keys.shape[1]
    heads_kv = cache_keys.shape[2] // HD
    shaped_q = queries.reshape(rows, steps, heads_kv, GQA, HD)
    keys_c = cache_keys.reshape(rows, length, heads_kv, HD)
    score_c = jnp.einsum(
        "rsgqd,rcgd->rgsqc", shaped_q, keys_c, preferred_element_type=jnp.float32
    ) * (1.0 / math.sqrt(HD))
    valid = jnp.arange(length, dtype=jnp.int32)[None, :] < cache_len[:, None]
    score_c = jnp.where(valid[:, None, None, None, :], score_c, -jnp.inf)
    return shaped_q, score_c, jnp.max(score_c, axis=-1)


def attend(shaped_q, score_c, top_c, causal, cache_values, new_keys, new_values):
    rows, steps, heads_kv = shaped_q.shape[:3]
    length = cache_values.shape[1]
    inverse = 1.0 / math.sqrt(HD)
    vals_c = cache_values.reshape(rows, length, heads_kv, HD)
    keys_n = new_keys.reshape(rows, steps, heads_kv, HD)
    vals_n = new_values.reshape(rows, steps, heads_kv, HD)
    score_n = (
        jnp.einsum("rsgqd,rtgd->rgsqt", shaped_q, keys_n, preferred_element_type=jnp.float32)
        * inverse
    )
    score_n = jnp.where(causal[None, None, :, None, :], score_n, -jnp.inf)
    top = jnp.maximum(top_c, jnp.max(score_n, axis=-1))
    exp_c = jnp.exp(score_c - top[..., None])
    exp_n = jnp.exp(score_n - top[..., None])
    total = jnp.sum(exp_c, axis=-1) + jnp.sum(exp_n, axis=-1)
    probs_c = (exp_c / total[..., None]).astype(jnp.bfloat16)
    probs_n = (exp_n / total[..., None]).astype(jnp.bfloat16)
    mixed = jnp.einsum("rgsqc,rcgd->rsgqd", probs_c, vals_c, preferred_element_type=jnp.float32)
    mixed = mixed + jnp.einsum(
        "rgsqt,rtgd->rsgqd", probs_n, vals_n, preferred_element_type=jnp.float32
    )
    return mixed.astype(jnp.bfloat16).reshape(rows, steps, -1)


def pick(target, size):
    c = lax.broadcasted_iota(jnp.int32, (len(target), size), 1)
    return (jnp.asarray(target, jnp.int32)[:, None] == c).astype(jnp.bfloat16)


def gradient_kernel(len_ref, adv_ref, act_ref, cot_ref, out_hbm, wgt_ref, out_ref, sem):
    tok_rows, quarter_rows = act_ref.shape
    parts = quarter_rows // CHUNK
    rest = out_ref.shape[0] - quarter_rows
    out_ref[quarter_rows:, :] = jnp.zeros((rest, out_ref.shape[1]), jnp.bfloat16)
    group = lax.axis_index(("x", "y", "z"))
    length = len_ref[group]
    adv = adv_ref[group].astype(jnp.float32)
    within = lax.broadcasted_iota(jnp.int32, (tok_rows, HD), 0)
    scale = jnp.where(within < length, adv / 256.0, jnp.float32(0.0)) / len_ref.shape[0]
    for c in range(cot_ref.shape[1] // HD):
        cols = pl.ds(c * HD, HD)
        wgt_ref[:, cols] = (cot_ref[:, cols].astype(jnp.float32) * scale).astype(jnp.bfloat16)
    stores = []
    for i in range(parts):
        out_ref[i * CHUNK : (i + 1) * CHUNK, :] = lax.dot_general(
            act_ref[:, i * CHUNK : (i + 1) * CHUNK],
            wgt_ref[...],
            (((0,), (0,)), ((), ())),
            preferred_element_type=jnp.float32,
        ).astype(jnp.bfloat16)
        end = (i + 1) * CHUNK if i + 1 < parts else out_ref.shape[0]
        rows = pl.ds(i * CHUNK, end - i * CHUNK)
        stores.append(pltpu.make_async_copy(out_ref.at[rows], out_hbm.at[rows], sem.at[i]))
        stores[i].start()
    for i in range(parts):
        stores[i].wait()


def blocks_kernel(got_ref, hidden_ref, out_ref):
    total = got_ref[0].astype(jnp.float32)
    for i in range(1, NX):
        total = total + got_ref[i].astype(jnp.float32)
    rows, own = out_ref.shape[0], got_ref.shape[1]
    r = lax.broadcasted_iota(jnp.int32, (rows, own), 0)
    c = lax.broadcasted_iota(jnp.int32, (rows, own), 1)
    block = r // PAD
    keep = ((block % NY * NZ + block // NY) * OWN + r % PAD == c) & (r % PAD < OWN)
    body = jnp.dot(
        keep.astype(jnp.bfloat16), total.astype(jnp.bfloat16), preferred_element_type=jnp.float32
    )
    count = hidden_ref.shape[0]
    r = lax.broadcasted_iota(jnp.int32, (rows, count), 0)
    c = lax.broadcasted_iota(jnp.int32, (rows, count), 1)
    last = r == c * PAD + OWN
    body = body + jnp.dot(
        last.astype(jnp.bfloat16), hidden_ref[...], preferred_element_type=jnp.float32
    )
    out_ref[...] = body.astype(jnp.bfloat16)


def shards(
    activations,
    cotangent,
    advantage,
    seq_len,
    key_master,
    moment_one,
    moment_two,
    decode_hidden,
    queries,
    cache_keys,
    cache_values,
    cache_len,
    value_weight,
):
    bf16, f32 = jnp.bfloat16, jnp.float32
    tok_rows, quarter_rows = activations.shape
    padded_rows = OWN * NX * NY * NZ
    width = cotangent.shape[1]
    smem = pl.BlockSpec(memory_space=pltpu.SMEM)
    vmem = pl.BlockSpec(memory_space=pltpu.VMEM)
    small = pltpu.CompilerParams(vmem_limit_bytes=16 * 2**20)
    partial = pl.pallas_call(
        gradient_kernel,
        out_shape=jax.ShapeDtypeStruct((padded_rows, width), bf16),
        in_specs=[smem, smem, vmem, vmem],
        out_specs=pl.BlockSpec(memory_space=pl.ANY),
        scratch_shapes=[
            pltpu.VMEM((tok_rows, width), bf16),
            pltpu.VMEM((padded_rows, width), bf16),
            pltpu.SemaphoreType.DMA((quarter_rows // CHUNK,)),
        ],
        name="gradient",
    )(seq_len, advantage, activations, cotangent)

    steps = decode_hidden.shape[1]
    by_quarter = jnp.pad(
        decode_hidden.reshape(steps * TP, quarter_rows), ((0, 0), (0, padded_rows - quarter_rows))
    )
    blocks = NY * NZ
    lanes = NX * PAD
    r = np.arange(padded_rows)
    block = r // OWN % NZ * NY + r // (OWN * NZ) % NY
    spread = pick(
        block * lanes + r // (OWN * blocks) * PAD + r % OWN, blocks * lanes
    )
    placed_h = jnp.dot(by_quarter, spread, preferred_element_type=f32).astype(bf16)
    placed_h = placed_h.reshape(steps * TP, blocks, lanes).transpose(1, 0, 2).reshape(blocks, width)

    got = lax.all_to_all(partial, "x", 0, 0, tiled=True)
    flat_hidden = decode_hidden.reshape(steps, -1)
    new_values = jnp.dot(flat_hidden, value_weight, preferred_element_type=f32).astype(bf16)[None]
    shaped_q, score_c, top_c = cache_scores(queries, cache_keys, cache_len)
    causal = (
        jnp.arange(steps, dtype=jnp.int32)[None, :] <= jnp.arange(steps, dtype=jnp.int32)[:, None]
    )
    got, placed_h, new_values, score_c, top_c, causal = lax.optimization_barrier(
        (got, placed_h, new_values, score_c, top_c, causal)
    )
    part_x = pl.pallas_call(
        blocks_kernel,
        out_shape=jax.ShapeDtypeStruct((blocks * PAD, width), bf16),
        in_specs=[vmem, vmem],
        out_specs=vmem,
        compiler_params=small,
        name="blocks",
    )(got.reshape(NX, blocks * OWN, width), placed_h)
    got = lax.all_to_all(part_x, ("z", "y"), 0, 0, tiled=True).reshape(blocks, PAD, width)
    gradient = jnp.sum(got[:, :OWN].astype(f32), axis=0).reshape(key_master.shape)
    hidden_yz = got[:, OWN].reshape(blocks * steps, TP * lanes)

    corr_one = 1.0 - 0.9**10
    corr_two = 1.0 - 0.95**10
    moment_one_new = 0.9 * moment_one + 0.1 * gradient
    moment_two_new = 0.95 * moment_two + 0.05 * gradient * gradient
    master_new = key_master - 0.005 * (moment_one_new / corr_one) / (
        jnp.sqrt(moment_two_new / corr_two) + 1e-08
    )
    relay = jnp.pad(master_new[0].astype(bf16), ((0, PAD - OWN), (0, 0)))

    heads = relay.reshape(PAD, TP, HD).transpose(1, 0, 2)
    send = jnp.broadcast_to(heads[:, None], (TP, NX, PAD, HD)).reshape(-1, HD)
    send, hidden_yz = lax.optimization_barrier((send, hidden_yz))
    weight = lax.all_to_all(send, ("h", "c", "x"), 0, 0, tiled=True)
    keys_yz = jnp.dot(hidden_yz, weight, preferred_element_type=f32)
    got = lax.all_to_all(keys_yz.reshape(blocks, steps, HD), ("z", "y"), 0, 0, tiled=True)
    new_keys = jnp.sum(got, axis=0).astype(bf16)[None]

    attention = attend(shaped_q, score_c, top_c, causal, cache_values, new_keys, new_values)
    return (master_new, moment_one_new, moment_two_new, new_keys, new_values, attention)


def solution(mesh):
    grid = Mesh(mesh.devices.reshape(NX, NY, NZ, 2, 2), ("x", "y", "z", "h", "c"))
    grp, tp = ("x", "y", "z"), ("h", "c")
    placed = (
        P(grp, tp),
        P(grp, None),
        P(),
        P(),
        P(tp, grp, None),
        P(tp, grp, None),
        P(tp, grp, None),
        P(grp, None, None),
        P(grp, None, tp),
        P(grp, None, tp),
        P(grp, None, tp),
        P(grp),
        P(None, tp),
    )
    return jax.shard_map(
        shards,
        mesh=grid,
        in_specs=placed,
        out_specs=(
            P(tp, grp, None),
            P(tp, grp, None),
            P(tp, grp, None),
            P(grp, None, tp),
            P(grp, None, tp),
            P(grp, None, tp),
        ),
        check_vma=False,
    )
```

```python
import math

import jax
import jax.numpy as jnp
import numpy as np
from jax import lax
from jax.experimental import pallas as pl
from jax.experimental.pallas import tpu as pltpu
from jax.sharding import Mesh, PartitionSpec as P

HD = 128
GQA = 5
SEQ = 256
NX, NY, NZ = 4, 4, 12
OWN = 7
PAD = 8
TP = 4
CHUNK = 256


def cache_scores(queries, cache_keys, cache_len):
    rows, steps, width = queries.shape
    length = cache_keys.shape[1]
    heads_kv = cache_keys.shape[2] // HD
    shaped_q = queries.reshape(rows, steps, heads_kv, GQA, HD)
    keys_c = cache_keys.reshape(rows, length, heads_kv, HD)
    score_c = jnp.einsum(
        "rsgqd,rcgd->rgsqc", shaped_q, keys_c, preferred_element_type=jnp.float32
    ) * (1.0 / math.sqrt(HD))
    valid = jnp.arange(length, dtype=jnp.int32)[None, :] < cache_len[:, None]
    score_c = jnp.where(valid[:, None, None, None, :], score_c, -jnp.inf)
    return shaped_q, score_c, jnp.max(score_c, axis=-1)


def attend(shaped_q, score_c, top_c, causal, cache_values, new_keys, new_values):
    rows, steps, heads_kv = shaped_q.shape[:3]
    length = cache_values.shape[1]
    inverse = 1.0 / math.sqrt(HD)
    vals_c = cache_values.reshape(rows, length, heads_kv, HD)
    keys_n = new_keys.reshape(rows, steps, heads_kv, HD)
    vals_n = new_values.reshape(rows, steps, heads_kv, HD)
    score_n = (
        jnp.einsum("rsgqd,rtgd->rgsqt", shaped_q, keys_n, preferred_element_type=jnp.float32)
        * inverse
    )
    score_n = jnp.where(causal[None, None, :, None, :], score_n, -jnp.inf)
    top = jnp.maximum(top_c, jnp.max(score_n, axis=-1))
    exp_c = jnp.exp(score_c - top[..., None])
    exp_n = jnp.exp(score_n - top[..., None])
    total = jnp.sum(exp_c, axis=-1) + jnp.sum(exp_n, axis=-1)
    probs_c = (exp_c / total[..., None]).astype(jnp.bfloat16)
    probs_n = (exp_n / total[..., None]).astype(jnp.bfloat16)
    mixed = jnp.einsum("rgsqc,rcgd->rsgqd", probs_c, vals_c, preferred_element_type=jnp.float32)
    mixed = mixed + jnp.einsum(
        "rgsqt,rtgd->rsgqd", probs_n, vals_n, preferred_element_type=jnp.float32
    )
    return mixed.astype(jnp.bfloat16).reshape(rows, steps, -1)


def pick(target, size):
    c = lax.broadcasted_iota(jnp.int32, (len(target), size), 1)
    return (jnp.asarray(target, jnp.int32)[:, None] == c).astype(jnp.bfloat16)


def gradient_kernel(len_ref, adv_ref, act_ref, cot_ref, out_hbm, wgt_ref, out_ref, sem):
    tok_rows, quarter_rows = act_ref.shape
    parts = quarter_rows // CHUNK
    rest = out_ref.shape[0] - quarter_rows
    out_ref[quarter_rows:, :] = jnp.zeros((rest, out_ref.shape[1]), jnp.bfloat16)
    group = lax.axis_index(("x", "y", "z"))
    length = len_ref[group]
    adv = adv_ref[group].astype(jnp.float32)
    within = lax.broadcasted_iota(jnp.int32, (tok_rows, HD), 0)
    scale = jnp.where(within < length, adv / 256.0, jnp.float32(0.0)) / len_ref.shape[0]
    for c in range(cot_ref.shape[1] // HD):
        cols = pl.ds(c * HD, HD)
        wgt_ref[:, cols] = (cot_ref[:, cols].astype(jnp.float32) * scale).astype(jnp.bfloat16)
    stores = []
    for i in range(parts):
        out_ref[i * CHUNK : (i + 1) * CHUNK, :] = lax.dot_general(
            act_ref[:, i * CHUNK : (i + 1) * CHUNK],
            wgt_ref[...],
            (((0,), (0,)), ((), ())),
            preferred_element_type=jnp.float32,
        ).astype(jnp.bfloat16)
        end = (i + 1) * CHUNK if i + 1 < parts else out_ref.shape[0]
        rows = pl.ds(i * CHUNK, end - i * CHUNK)
        stores.append(pltpu.make_async_copy(out_ref.at[rows], out_hbm.at[rows], sem.at[i]))
        stores[i].start()
    for i in range(parts):
        stores[i].wait()


def blocks_kernel(got_ref, hidden_ref, out_ref):
    total = got_ref[0].astype(jnp.float32)
    for i in range(1, NX):
        total = total + got_ref[i].astype(jnp.float32)
    rows, own = out_ref.shape[0], got_ref.shape[1]
    r = lax.broadcasted_iota(jnp.int32, (rows, own), 0)
    c = lax.broadcasted_iota(jnp.int32, (rows, own), 1)
    block = r // PAD
    keep = ((block % NY * NZ + block // NY) * OWN + r % PAD == c) & (r % PAD < OWN)
    body = jnp.dot(
        keep.astype(jnp.bfloat16), total.astype(jnp.bfloat16), preferred_element_type=jnp.float32
    )
    count = hidden_ref.shape[0]
    r = lax.broadcasted_iota(jnp.int32, (rows, count), 0)
    c = lax.broadcasted_iota(jnp.int32, (rows, count), 1)
    last = r == c * PAD + OWN
    body = body + jnp.dot(
        last.astype(jnp.bfloat16), hidden_ref[...], preferred_element_type=jnp.float32
    )
    out_ref[...] = body.astype(jnp.bfloat16)


def shards(
    activations,
    cotangent,
    advantage,
    seq_len,
    key_master,
    moment_one,
    moment_two,
    decode_hidden,
    queries,
    cache_keys,
    cache_values,
    cache_len,
    value_weight,
):
    bf16, f32 = jnp.bfloat16, jnp.float32
    tok_rows, quarter_rows = activations.shape
    padded_rows = OWN * NX * NY * NZ
    width = cotangent.shape[1]
    smem = pl.BlockSpec(memory_space=pltpu.SMEM)
    vmem = pl.BlockSpec(memory_space=pltpu.VMEM)
    small = pltpu.CompilerParams(vmem_limit_bytes=16 * 2**20)
    partial = pl.pallas_call(
        gradient_kernel,
        out_shape=jax.ShapeDtypeStruct((padded_rows, width), bf16),
        in_specs=[smem, smem, vmem, vmem],
        out_specs=pl.BlockSpec(memory_space=pl.ANY),
        scratch_shapes=[
            pltpu.VMEM((tok_rows, width), bf16),
            pltpu.VMEM((padded_rows, width), bf16),
            pltpu.SemaphoreType.DMA((quarter_rows // CHUNK,)),
        ],
        name="gradient",
    )(seq_len, advantage, activations, cotangent)

    steps = decode_hidden.shape[1]
    by_quarter = jnp.pad(
        decode_hidden.reshape(steps * TP, quarter_rows), ((0, 0), (0, padded_rows - quarter_rows))
    )
    blocks = NY * NZ
    lanes = NX * PAD
    r = np.arange(padded_rows)
    block = r // OWN % NZ * NY + r // (OWN * NZ) % NY
    spread = pick(
        block * lanes + r // (OWN * blocks) * PAD + r % OWN, blocks * lanes
    )
    placed_h = jnp.dot(by_quarter, spread, preferred_element_type=f32).astype(bf16)
    placed_h = placed_h.reshape(steps * TP, blocks, lanes).transpose(1, 0, 2).reshape(blocks, width)

    got = lax.all_to_all(partial, "x", 0, 0, tiled=True)
    flat_hidden = decode_hidden.reshape(steps, -1)
    new_values = jnp.dot(flat_hidden, value_weight, preferred_element_type=f32).astype(bf16)[None]
    shaped_q, score_c, top_c = cache_scores(queries, cache_keys, cache_len)
    causal = (
        jnp.arange(steps, dtype=jnp.int32)[None, :] <= jnp.arange(steps, dtype=jnp.int32)[:, None]
    )
    got, placed_h, new_values, score_c, top_c, causal = lax.optimization_barrier(
        (got, placed_h, new_values, score_c, top_c, causal)
    )
    part_x = pl.pallas_call(
        blocks_kernel,
        out_shape=jax.ShapeDtypeStruct((blocks * PAD, width), bf16),
        in_specs=[vmem, vmem],
        out_specs=vmem,
        compiler_params=small,
        name="blocks",
    )(got.reshape(NX, blocks * OWN, width), placed_h)
    got = lax.all_to_all(part_x, ("z", "y"), 0, 0, tiled=True).reshape(blocks, PAD, width)
    gradient = jnp.sum(got[:, :OWN].astype(f32), axis=0).reshape(key_master.shape)
    hidden_yz = got[:, OWN].reshape(blocks * steps, TP * lanes)

    corr_one = 1.0 - 0.9**10
    corr_two = 1.0 - 0.95**10
    moment_one_new = 0.9 * moment_one + 0.1 * gradient
    moment_two_new = 0.95 * moment_two + 0.05 * gradient * gradient
    master_new = key_master - 0.005 * (moment_one_new / corr_one) / (
        jnp.sqrt(moment_two_new / corr_two) + 1e-08
    )
    relay = jnp.pad(master_new[0].astype(bf16), ((0, PAD - OWN), (0, 0)))

    heads = relay.reshape(PAD, TP, HD).transpose(1, 0, 2)
    send = jnp.broadcast_to(heads[None], (NX, TP, PAD, HD)).reshape(-1, HD)
    send, hidden_yz = lax.optimization_barrier((send, hidden_yz))
    got = lax.all_to_all(send, ("x", "h", "c"), 0, 0, tiled=True)
    weight = got.reshape(NX, TP, PAD, HD).transpose(1, 0, 2, 3).reshape(-1, HD)
    keys_yz = jnp.dot(hidden_yz, weight, preferred_element_type=f32)
    got = lax.all_to_all(keys_yz.reshape(blocks, steps, HD), ("z", "y"), 0, 0, tiled=True)
    new_keys = jnp.sum(got, axis=0).astype(bf16)[None]

    attention = attend(shaped_q, score_c, top_c, causal, cache_values, new_keys, new_values)
    return (master_new, moment_one_new, moment_two_new, new_keys, new_values, attention)


def solution(mesh):
    grid = Mesh(mesh.devices.reshape(NX, NY, NZ, 2, 2), ("x", "y", "z", "h", "c"))
    grp, tp = ("x", "y", "z"), ("h", "c")
    placed = (
        P(grp, tp),
        P(grp, None),
        P(),
        P(),
        P(tp, grp, None),
        P(tp, grp, None),
        P(tp, grp, None),
        P(grp, None, None),
        P(grp, None, tp),
        P(grp, None, tp),
        P(grp, None, tp),
        P(grp),
        P(None, tp),
    )
    return jax.shard_map(
        shards,
        mesh=grid,
        in_specs=placed,
        out_specs=(
            P(tp, grp, None),
            P(tp, grp, None),
            P(tp, grp, None),
            P(grp, None, tp),
            P(grp, None, tp),
            P(grp, None, tp),
        ),
        check_vma=False,
    )
```
